32 devices in a mesh: row: 8 (over y, x, core), col: 4 (over z).
Axes of the slice: x: 2, y: 2, z: 4, core: 2. Of those that a mesh axis runs over, the one named last changes fastest.
Arguments:
- voltage: bfloat16 [8, 4, 2048, 256], P('row', 'col'), may hold values from -6 to 6
- sources: bfloat16 [8, 4, 2048, 256], P('row', 'col'), may hold values from -6 to 6
- capacity: float32 [8, 4, 2048], P('row', 'col'), may hold values from 0.1 to 1
- inverse: bfloat16 [8, 4, 2048, 2048], P('row', 'col')
- couple: bfloat16 [8, 4, 256, 1024], P('row', 'col'), may hold values from -0.1875 to 0.1875
- boundary: int32 [8, 4, 256], P('row', 'col'), may hold values from 0 to 2047, as said below
- panels: bfloat16 [8, 4, 5, 16, 3, 128, 128], P('row', 'col'), may hold values from -0.125 to 0.125
- pattern: int32 [8, 4, 5, 16, 3], P('row', 'col'), may hold values from 0 to 15
Outputs:
- settled: float32 [8, 4, 2048, 256], P('row', 'col')
The draws below stay inside these ranges and needn't reach their ends.
Inputs may be any that keep to these rules, and one draw needn't show every extreme that they name: `boundary`: the 256 indices of one subdomain are distinct.
All inputs are finite; a program needn't handle non-finite values.
Results may differ from the reference program's by a relative error of at most 0.007.
Values may be sent and summed in bfloat16 or wider, within the bound.
A program may use at most 128 MiB of HBM per device.

```python
import math
import jax
import jax.numpy as jnp
from jax import lax

NI = 2048
BLK = 128
KB = 3
NBND = 256
RHS = 256
STEPS = 2
NB = 16
LEVELS = 5
N_ROW = 8
N_COL = 4


def draw_inverse(key, part):
    key_off = jax.random.fold_in(key, 11)
    key_diag = jax.random.fold_in(key, 12)
    shape = (N_ROW, N_COL, NI, NI)
    off = jax.random.normal(key_off, shape, jnp.float32) * (0.4 / NI ** 0.5)
    diag = jax.random.uniform(key_diag, (N_ROW, N_COL, NI), jnp.float32, 0.3, 0.6)
    eye = jnp.eye(NI, dtype=jnp.float32)
    full = off + diag[..., None] * eye
    return full.astype(jnp.bfloat16)


def draw_boundary(key, part):
    keys = jax.random.split(jax.random.fold_in(key, 21), N_ROW * N_COL)
    picked = jax.vmap(lambda one: jax.random.permutation(one, NI)[:NBND])(keys)
    return picked.reshape(N_ROW, N_COL, NBND).astype(jnp.int32)


def place_ends(entries, rng, least, top_value):
    extent = entries.shape
    place = [jax.random.randint(jax.random.fold_in(rng, axis), (), 0, extent[axis]) for axis in range(len(extent))]
    entries = entries.at[tuple(place)].set(least)
    longest = extent.index(max(extent))
    place[longest] = (place[longest] + 1) % extent[longest]
    return entries.at[tuple(place)].set(top_value)


def block_scale(key, dims, pieces, smallest, top_value):
    def one(position, parts):
        draws = jax.random.uniform(jax.random.fold_in(jax.random.fold_in(key, 6), position), (parts,), jnp.float32, smallest / len(pieces), top_value / len(pieces))
        return jnp.repeat(jnp.exp(draws), dims[position] // parts).reshape((-1,) + (1,) * (len(dims) - position - 1))

    level = one(*pieces[0])
    for cut in pieces[1:]:
        level = level * one(*cut)
    return level


def noise(key, extent, deviation, bound, cuts=(), held_as=jnp.bfloat16):
    factor_of = block_scale(key, extent, cuts, -0.22, 0.18) if cuts else 1.0
    drawn = jax.random.normal(key, extent, jnp.float32) * deviation * factor_of
    return jnp.minimum(jnp.maximum(drawn, -bound), bound).astype(held_as)


def setup_inputs(seed: int = 0) -> dict:
    splits = jax.random.split(jax.random.key(seed), 9)
    voltage = noise(splits[0], (N_ROW, N_COL, NI, RHS), 1.0, 6.0, ((0, 8), (1, 4)))
    sources = noise(splits[1], (N_ROW, N_COL, NI, RHS), 1.0, 6.0, ((0, 8), (1, 4)))
    capacity = jnp.clip(jnp.exp(math.log(1.0) - 2.3025851 * jax.random.uniform(splits[2], (N_ROW, N_COL, NI), jnp.float32) ** block_scale(splits[2], (N_ROW, N_COL, NI), ((0, 8), (1, 4)), -0.2, 0.2)), 0.1, 1.0)
    inverse = draw_inverse(jax.random.fold_in(splits[8], 71), 0)
    couple = noise(splits[4], (N_ROW, N_COL, NBND, N_COL * NBND), (N_COL * NBND) ** -0.5, 0.1875, ((0, 8), (1, 4)))
    boundary = draw_boundary(jax.random.fold_in(splits[8], 71), 0)
    panels = noise(splits[6], (N_ROW, N_COL, LEVELS, NB, KB, BLK, BLK), (KB * BLK * 6) ** -0.5, 0.125, ((0, 8), (1, 4)))
    pattern = place_ends(jax.random.randint(splits[7], (N_ROW, N_COL, LEVELS, NB, KB), 0, NB), jax.random.fold_in(splits[7], 1), 0, NB - 1).astype(jnp.int32)
    return {"voltage": voltage, "sources": sources, "capacity": capacity, "inverse": inverse, "couple": couple, "boundary": boundary, "panels": panels, "pattern": pattern}


def merge_level(merged, panels_level, pattern_level, level):
    devices = N_ROW * N_COL
    stride = 2 ** level
    sent = merged.astype(jnp.bfloat16)
    partner = sent.reshape(devices // (2 * stride), 2, stride, NI, RHS)[:, ::-1].reshape(devices, NI, RHS)

    def apply_panel(items):
        received, blocks, columns = items
        tiles = received.reshape(NB, BLK, RHS)
        picked = tiles[columns].astype(jnp.float32)
        update = jnp.einsum("nkij,nkjr->nir", blocks.astype(jnp.float32), picked)
        return update.reshape(NI, RHS)

    update = lax.map(apply_panel, (partner, panels_level, pattern_level))
    return merged + update


def reference(voltage, sources, capacity, inverse, couple, boundary, panels, pattern):
    devices = N_ROW * N_COL
    potential = voltage.astype(jnp.float32).reshape(devices, NI, RHS)
    source_flat = sources.astype(jnp.float32).reshape(devices, NI, RHS)
    cap_flat = capacity.reshape(devices, NI, 1)
    index_flat = boundary.reshape(devices, NBND).astype(jnp.int32)
    inverse_flat = inverse.reshape(devices, NI, NI)
    panel_flat = panels.reshape(devices, LEVELS, NB, KB, BLK, BLK)
    pattern_flat = pattern.reshape(devices, LEVELS, NB, KB).astype(jnp.int32)
    weights = couple.astype(jnp.float32)
    device_ids = jnp.arange(devices, dtype=jnp.int32)[:, None]
    for step in range(STEPS):
        edge = potential[device_ids, index_flat].astype(jnp.bfloat16)
        edge_rows = edge.reshape(N_ROW, N_COL * NBND, RHS).astype(jnp.float32)
        coupled = jnp.einsum("rcbk,rkn->rcbn", weights, edge_rows).reshape(devices, NBND, RHS)
        base = cap_flat * potential + source_flat
        loaded = base.at[device_ids, index_flat].add(coupled).astype(jnp.bfloat16)
        merged = lax.map(lambda items: jnp.dot(items[0], items[1], preferred_element_type=jnp.float32), (inverse_flat, loaded))
        for level in range(LEVELS):
            merged = merge_level(merged, panel_flat[:, level], pattern_flat[:, level], level)
        potential = merged
    return potential.reshape(N_ROW, N_COL, NI, RHS)
```

```python
import functools

import jax
import jax.numpy as jnp
from jax import lax
from jax.experimental import pallas as pl
from jax.experimental.pallas import tpu as pltpu
from jax.sharding import PartitionSpec as P

STEPS = 2
CHUNKS = 2
PIECES = 4
F32 = jnp.float32
BF16 = jnp.bfloat16
MESH = pl.DeviceIdType.MESH


def plan(levels, col_levels):
    wire = [10.0 * 2**bit for bit in range(col_levels)]
    wire += [2.0] + [10.0] * (levels - col_levels - 1)
    wire = [t * 2 / CHUNKS for t in wire]
    stages = [(s, t) for s in range(STEPS) for t in range(-2, levels)]
    at = [0] * CHUNKS
    ready = [0.0] * CHUNKS
    links = {}
    now = 0.0
    order = []
    while any(at[c] < len(stages) for c in range(CHUNKS)):
        left = [c for c in range(CHUNKS) if at[c] < len(stages)]
        c = min(left, key=lambda k: (max(ready[k], now), k))
        s, t = stages[at[c]]
        at[c] += 1
        order.append((s, t, c))
        now = max(now, ready[c]) + (4.0 if t == -1 else 1.0)
        if t == levels - 1:
            ready[c] = now
        else:
            nxt = t + 1
            key = "z" if nxt < col_levels else nxt
            cost = 1.0 if t == -2 else wire[nxt]
            start = max(now, links.get(key, 0.0)) if t != -2 else now
            links[key] = start + cost
            ready[c] = start + cost + 1.5
    return order


def kernel(
    ncol, nrow, levels, nb, kb, blk, nbnd, rhs,
    cap_ref, bnd_ref, pat_ref, volt_hbm, src_hbm, inv_hbm, cpl_hbm, pan_hbm,
    out_hbm, *scratch,
):
    ni = nb * blk
    w = rhs // CHUNKS
    col_levels = ncol.bit_length() - 1
    (inv, pan, cpl, src, capb, hot, hot_t, load_sem, out_sem,
     gs_sem, gr_sem, ls_sem, lr_sem) = scratch[:13]
    rest = list(scratch[13:])
    merged = [rest.pop(0) for _ in range(CHUNKS)]
    low = [rest.pop(0) for _ in range(CHUNKS)]
    loaded = [rest.pop(0) for _ in range(CHUNKS)]
    edges = [[rest.pop(0) for _ in range(CHUNKS)] for _ in range(STEPS)]
    got = [[[rest.pop(0) for _ in range(CHUNKS)] for _ in range(levels)] for _ in range(STEPS)]

    loads = []
    for c in range(CHUNKS):
        cols = pl.ds(c * w, w)
        for p in range(nb):
            loads.append(pltpu.make_async_copy(
                volt_hbm.at[0, 0, pl.ds(p * blk, blk), cols], low[c].at[p], load_sem.at[0, c, p]))
    volt_loads = loads
    src_loads = [pltpu.make_async_copy(src_hbm.at[0, 0, :, pl.ds(c * w, w)], src.at[c], load_sem.at[1, c, 0]) for c in range(CHUNKS)]
    cpl_load = pltpu.make_async_copy(cpl_hbm.at[0, 0], cpl, load_sem.at[1, 0, 1])
    rows_each = ni // PIECES
    inv_loads = [pltpu.make_async_copy(inv_hbm.at[0, 0, pl.ds(p * rows_each, rows_each)], inv.at[pl.ds(p * rows_each, rows_each)], load_sem.at[1, 1, 1 + p]) for p in range(PIECES)]
    pan_loads = [pltpu.make_async_copy(pan_hbm.at[0, 0, l], pan.at[l], load_sem.at[1, 0, 2 + l]) for l in range(levels)]
    for one in volt_loads + [cpl_load] + src_loads + inv_loads + pan_loads:
        one.start()

    my_row = lax.axis_index("row")
    my_col = lax.axis_index("col")

    def flip(me, mask):
        return me + mask - 2 * mask * lax.rem(me // mask, 2)

    partners = []
    for l in range(levels):
        if l < col_levels:
            partners.append((my_row, flip(my_col, 2**l)))
        else:
            partners.append((flip(my_row, 2 ** (l - col_levels)), my_col))
    barrier = pltpu.get_barrier_semaphore()
    for o in range(1, ncol):
        pl.semaphore_signal(barrier, inc=1, device_id=(my_row, lax.rem(my_col + o, ncol)), device_id_type=MESH)
    for l in range(col_levels, levels):
        pl.semaphore_signal(barrier, inc=1, device_id=partners[l], device_id_type=MESH)

    bnd_row = bnd_ref[...]
    bnd_col = jnp.transpose(jnp.broadcast_to(bnd_row.astype(F32), (blk, nbnd)))
    for j in range(nb):
        rows = lax.broadcasted_iota(jnp.int32, (blk, nbnd), 0) + j * blk
        hot[pl.ds(j * blk, blk), :] = jnp.where(rows == bnd_row, 1.0, 0.0).astype(BF16)
        lanes = (lax.broadcasted_iota(jnp.int32, (nbnd, blk), 1) + j * blk).astype(F32)
        hot_t[:, pl.ds(j * blk, blk)] = jnp.where(lanes == bnd_col, 1.0, 0.0).astype(BF16)
        capb[pl.ds(j * blk, blk), :] = jnp.transpose(
            jnp.broadcast_to(cap_ref[:, pl.ds(j * blk, blk)], (blk, blk)))[:, :w]

    pl.semaphore_wait(barrier, ncol - 1 + levels - col_levels)

    def edge_copy(s, c, o):
        return pltpu.make_async_remote_copy(
            src_ref=edges[s][c].at[my_col], dst_ref=edges[s][c].at[my_col],
            send_sem=gs_sem.at[s, c, o], recv_sem=gr_sem.at[s, c, o],
            device_id=(my_row, lax.rem(my_col + o, ncol)), device_id_type=MESH)

    per = nb // PIECES

    def level_copy(s, l, c, p):
        return pltpu.make_async_remote_copy(
            src_ref=low[c].at[pl.ds(p * per, per)], dst_ref=got[s][l][c].at[pl.ds(p * per, per)],
            send_sem=ls_sem.at[s, l, c, p], recv_sem=lr_sem.at[s, l, c, p],
            device_id=partners[l], device_id_type=MESH)

    def out_copy(c, p):
        rows = pl.ds(p * rows_each, rows_each)
        return pltpu.make_async_copy(merged[c].at[rows], out_hbm.at[0, 0, rows, pl.ds(c * w, w)], out_sem.at[c, p])

    def gather_stage(s, c):
        if s == 0:
            for p in range(nb):
                volt_loads[c * nb + p].wait()
        state = low[c][...].reshape(ni, w)
        edges[s][c][my_col] = jnp.dot(hot_t[...], state, preferred_element_type=F32).astype(BF16)
        for o in range(1, ncol):
            edge_copy(s, c, o).start()

    def interior_stage(s, c):
        if s == 0:
            src_loads[c].wait()
            if c == 0:
                cpl_load.wait()
        for o in range(1, ncol):
            edge_copy(s, c, o).wait()
        coupled = jnp.dot(cpl[...], edges[s][c][...].reshape(ncol * nbnd, w), preferred_element_type=F32)
        high = coupled.astype(BF16)
        rest_part = (coupled - high.astype(F32)).astype(BF16)
        both = jnp.concatenate([high, rest_part], axis=1)

        def load_rows(p, carry):
            rows = pl.ds(pl.multiple_of(p * rows_each, rows_each), rows_each)
            spread = jnp.dot(hot[rows, :], both, preferred_element_type=F32)
            if s == 0:
                pot = low[c][pl.ds(p * per, per)].reshape(rows_each, w).astype(F32)
            else:
                pot = merged[c][rows, :]
            base = capb[rows, :] * pot + src[c, rows, :].astype(F32)
            loaded[c][rows, :] = (base + (spread[:, :w] + spread[:, w:])).astype(BF16)
            return carry

        lax.fori_loop(0, PIECES, load_rows, 0)
        if s == 0 and c == 0:
            for one in inv_loads:
                one.wait()

        def inner(p, carry):
            rows = pl.ds(pl.multiple_of(p * rows_each, rows_each), rows_each)
            value = jnp.dot(inv[rows, :], loaded[c][...], preferred_element_type=F32)
            merged[c][rows, :] = value
            low[c][pl.ds(p * per, per)] = value.astype(BF16).reshape(per, blk, w)
            level_copy(s, 0, c, p).start()
            return carry

        lax.fori_loop(0, PIECES, inner, 0)

    def merge_stage(s, l, c):
        if s == 0 and c == 0:
            pan_loads[l].wait()
        for p in range(PIECES):
            level_copy(s, l, c, p).wait()
        final = s == STEPS - 1 and l == levels - 1

        def piece(p, carry):
            for u in range(per):
                i = p * per + u
                rows = pl.ds(pl.multiple_of(i * blk, blk), blk)
                left = jnp.concatenate([pan[l, i, k] for k in range(kb)], axis=1)
                right = jnp.concatenate([got[s][l][c][pat_ref[0, 0, l, i, k]] for k in range(kb)], axis=0)
                value = merged[c][rows, :] + jnp.dot(left, right, preferred_element_type=F32)
                merged[c][rows, :] = value
                if not final:
                    low[c][i] = value.astype(BF16)
            if l < levels - 1:
                level_copy(s, l + 1, c, p).start()
            elif final:
                out_copy(c, p).start()
            return carry

        lax.fori_loop(0, PIECES, piece, 0)

    for s, t, c in plan(levels, col_levels):
        if t == -2:
            gather_stage(s, c)
        elif t == -1:
            interior_stage(s, c)
        else:
            merge_stage(s, t, c)
    for c in range(CHUNKS):
        for p in range(PIECES):
            out_copy(c, p).wait()


def per_device(mesh, voltage, sources, capacity, inverse, couple, boundary, panels, pattern):
    ncol, nrow = mesh.shape["col"], mesh.shape["row"]
    _, _, levels, nb, kb, blk, _ = panels.shape
    ni, rhs = voltage.shape[2:]
    nbnd = boundary.shape[2]
    w = rhs // CHUNKS
    sems = pltpu.SemaphoreType.DMA
    scratch = [
        pltpu.VMEM((ni, ni), BF16),
        pltpu.VMEM((levels, nb, kb, blk, blk), BF16),
        pltpu.VMEM((nbnd, ncol * nbnd), BF16),
        pltpu.VMEM((CHUNKS, ni, w), BF16),
        pltpu.VMEM((ni, w), F32),
        pltpu.VMEM((ni, nbnd), BF16),
        pltpu.VMEM((nbnd, ni), BF16),
        sems((2, CHUNKS, nb)),
        sems((CHUNKS, PIECES)),
        sems((STEPS, CHUNKS, ncol)),
        sems((STEPS, CHUNKS, ncol)),
        sems((STEPS, levels, CHUNKS, PIECES)),
        sems((STEPS, levels, CHUNKS, PIECES)),
    ]
    scratch += [pltpu.VMEM((ni, w), F32) for _ in range(CHUNKS)]
    scratch += [pltpu.VMEM((nb, blk, w), BF16) for _ in range(CHUNKS)]
    scratch += [pltpu.VMEM((ni, w), BF16) for _ in range(CHUNKS)]
    scratch += [pltpu.VMEM((ncol, nbnd, w), BF16) for _ in range(STEPS * CHUNKS)]
    scratch += [pltpu.VMEM((nb, blk, w), BF16) for _ in range(STEPS * levels * CHUNKS)]
    vmem = pl.BlockSpec(memory_space=pltpu.VMEM)
    smem = pl.BlockSpec(memory_space=pltpu.SMEM)
    hbm = pl.BlockSpec(memory_space=pl.ANY)
    return pl.pallas_call(
        functools.partial(kernel, ncol, nrow, levels, nb, kb, blk, nbnd, rhs),
        out_shape=jax.ShapeDtypeStruct((1, 1, ni, rhs), F32),
        in_specs=[vmem, vmem, smem, hbm, hbm, hbm, hbm, hbm],
        out_specs=hbm,
        scratch_shapes=scratch,
        compiler_params=pltpu.CompilerParams(
            collective_id=0, has_side_effects=True, vmem_limit_bytes=67_043_328),
    )(capacity.reshape(1, ni), boundary.reshape(1, nbnd), pattern, voltage, sources, inverse, couple, panels)


def solution(mesh):
    return jax.shard_map(
        functools.partial(per_device, mesh),
        mesh=mesh,
        in_specs=(
            P("row", "col", None, None),
            P("row", "col", None, None),
            P("row", "col", None),
            P("row", "col", None, None),
            P("row", "col", None, None),
            P("row", "col", None),
            P("row", "col", None, None, None, None, None),
            P("row", "col", None, None, None),
        ),
        out_specs=P("row", "col", None, None),
        check_vma=False,
    )
```

```python
import functools

import jax
import jax.numpy as jnp
from jax import lax
from jax.experimental import pallas as pl
from jax.experimental.pallas import tpu as pltpu
from jax.sharding import PartitionSpec as P

STEPS = 2
CHUNKS = 4
PIECES = 4
F32 = jnp.float32
BF16 = jnp.bfloat16
MESH = pl.DeviceIdType.MESH


def plan(levels, col_levels):
    wire = [10.0 * 2**bit for bit in range(col_levels)]
    wire += [1.5] + [10.0] * (levels - col_levels - 1)
    wire = [t * 2 / CHUNKS for t in wire]
    stages = [(0, t) for t in range(levels)]
    stages += [(s, t) for s in range(1, STEPS) for t in range(-2, levels)]
    at = [0] * CHUNKS
    ready = [2.0 + wire[0] * (c + 1) for c in range(CHUNKS)]
    links = {"z": 0.0}
    now = 0.0
    order = []
    while any(at[c] < len(stages) for c in range(CHUNKS)):
        left = [c for c in range(CHUNKS) if at[c] < len(stages)]
        c = min(left, key=lambda k: (max(ready[k], now), at[k], k))
        s, t = stages[at[c]]
        at[c] += 1
        order.append((s, t, c))
        now = max(now, ready[c]) + {-2: 0.6, -1: 3.0}.get(t, 1.0)
        if t == levels - 1:
            ready[c] = now
        elif t == -2:
            ready[c] = now + 3.0
        else:
            nxt = t + 1
            key = nxt
            start = max(now, links.get(key, 0.0))
            links[key] = start + wire[nxt]
            ready[c] = start + wire[nxt] + 1.5
    return order


def kernel(
    ncol, nrow, levels, nb, kb, blk, nbnd, rhs,
    cap_ref, bnd_ref, pat_ref, volt_hbm, src_hbm, inv_hbm, cpl_hbm, pan_hbm,
    out_hbm, *scratch,
):
    ni = nb * blk
    w = rhs // CHUNKS
    half = nb // 2
    hrows = ni // 2
    hb = nbnd // 2
    col_levels = ncol.bit_length() - 1
    (inv, pan, cpl, volt, src, capb, hot, hot_t, outb, loaded0, loaded, tiles, edge0, load_sem, out_sem,
     gs_sem, gr_sem, ls_sem, lr_sem) = scratch[:19]
    rest = list(scratch[19:])
    merged = [rest.pop(0) for _ in range(CHUNKS)]
    low = [rest.pop(0) for _ in range(CHUNKS)]
    edges = [[rest.pop(0) for _ in range(CHUNKS)] for _ in range(STEPS - 1)]
    got = [[[rest.pop(0) for _ in range(CHUNKS)] for _ in range(levels)] for _ in range(STEPS)]

    rows_each = hrows // PIECES
    volt_load = pltpu.make_async_copy(volt_hbm.at[0, 0], volt, load_sem.at[0])
    src_load = pltpu.make_async_copy(src_hbm.at[0, 0], src, load_sem.at[1])
    cpl_load = pltpu.make_async_copy(cpl_hbm.at[0, 0], cpl, load_sem.at[2])
    inv_load = pltpu.make_async_copy(inv_hbm.at[0, 0], inv, load_sem.at[3])
    pan_loads = [pltpu.make_async_copy(pan_hbm.at[0, 0, l], pan.at[l], load_sem.at[4 + l]) for l in range(levels)]
    for one in [volt_load, cpl_load, src_load, inv_load] + pan_loads:
        one.start()

    my_row = lax.axis_index("row")
    my_col = lax.axis_index("col")

    def flip(me, mask):
        return me + mask - 2 * mask * lax.rem(me // mask, 2)

    partners = []
    for l in range(levels):
        if l < col_levels:
            partners.append((my_row, flip(my_col, 2**l)))
        else:
            partners.append((flip(my_row, 2 ** (l - col_levels)), my_col))
    barrier = pltpu.get_barrier_semaphore()
    for o in range(1, ncol):
        pl.semaphore_signal(barrier, inc=1, device_id=(my_row, lax.rem(my_col + o, ncol)), device_id_type=MESH)
    for l in range(col_levels, levels):
        pl.semaphore_signal(barrier, inc=1, device_id=partners[l], device_id_type=MESH)

    bnd_row = bnd_ref[...]
    bnd_col = jnp.transpose(jnp.broadcast_to(bnd_row.astype(F32), (blk, nbnd)))
    for j in range(nb):
        rows = lax.broadcasted_iota(jnp.int32, (blk, nbnd), 0) + j * blk
        hot[pl.ds(j * blk, blk), :] = jnp.where(rows == bnd_row, 1.0, 0.0).astype(BF16)
        lanes = (lax.broadcasted_iota(jnp.int32, (nbnd, blk), 1) + j * blk).astype(F32)
        hot_t[:, pl.ds(j * blk, blk)] = jnp.where(lanes == bnd_col, 1.0, 0.0).astype(BF16)
        capb[pl.ds(j * blk, blk), :] = jnp.transpose(
            jnp.broadcast_to(cap_ref[:, pl.ds(j * blk, blk)], (blk, blk)))

    pl.semaphore_wait(barrier, ncol - 1 + levels - col_levels)

    def edge_copy(s, c, o):
        ref = edge0 if s == 0 else edges[s - 1][c]
        return pltpu.make_async_remote_copy(
            src_ref=ref.at[my_col], dst_ref=ref.at[my_col],
            send_sem=gs_sem.at[s, c, o], recv_sem=gr_sem.at[s, c, o],
            device_id=(my_row, lax.rem(my_col + o, ncol)), device_id_type=MESH)

    per = half // PIECES

    def level_copy(s, l, c, p):
        return pltpu.make_async_remote_copy(
            src_ref=low[c].at[pl.ds(p * per, per)], dst_ref=got[s][l][c].at[pl.ds(p * per, per)],
            send_sem=ls_sem.at[s, l, c, p], recv_sem=lr_sem.at[s, l, c, p],
            device_id=partners[l], device_id_type=MESH)

    def out_copy(g, p):
        rows = pl.ds(p * (ni // PIECES), ni // PIECES)
        return pltpu.make_async_copy(
            outb.at[g, rows], out_hbm.at[0, 0, rows, pl.ds(g * blk, blk)], out_sem.at[g, p])

    def split_parts(coupled):
        high = coupled.astype(BF16)
        return high, (coupled - high.astype(F32)).astype(BF16)

    def first_step():
        volt_load.wait()
        edge0[my_col] = jnp.dot(hot_t[...], volt[...], preferred_element_type=F32).astype(BF16)
        for o in range(1, ncol):
            edge_copy(0, 0, o).start()
        src_load.wait()
        cpl_load.wait()
        for o in range(1, ncol):
            edge_copy(0, 0, o).wait()
        coupled = jnp.dot(cpl[...], edge0[...].reshape(ncol * nbnd, rhs), preferred_element_type=F32)
        both = jnp.concatenate(split_parts(coupled), axis=0)

        def load_rows(p, carry):
            rows = pl.ds(pl.multiple_of(p * rows_each, rows_each), rows_each)
            ones = hot[rows, :]
            spread = jnp.dot(jnp.concatenate([ones, ones], axis=1), both, preferred_element_type=F32)
            cap = capb[rows, :]
            base = jnp.concatenate([cap] * (rhs // blk), axis=1) * volt[rows, :].astype(F32) + src[rows, :].astype(F32)
            loaded0[rows, :] = (base + spread).astype(BF16)
            return carry

        lax.fori_loop(0, 2 * PIECES, load_rows, 0)
        inv_load.wait()

        def inner(p, carry):
            rows = pl.ds(pl.multiple_of(p * rows_each, rows_each), rows_each)
            under = pl.ds(pl.multiple_of(p * rows_each, rows_each) + hrows, rows_each)
            top = jnp.dot(inv[rows, :], loaded0[...], preferred_element_type=F32)
            bottom = jnp.dot(inv[under, :], loaded0[...], preferred_element_type=F32)
            for c in range(CHUNKS):
                value = jnp.concatenate([top[:, c * w:(c + 1) * w], bottom[:, c * w:(c + 1) * w]], axis=1)
                merged[c][rows, :] = value
                low[c][pl.ds(p * per, per)] = value.astype(BF16).reshape(per, blk, blk)
            level_copy(0, 0, 0, p).start()
            return carry

        lax.fori_loop(0, PIECES, inner, 0)
        for c in range(1, CHUNKS):
            for p in range(PIECES):
                level_copy(0, 0, c, p).start()

    def gather_stage(s, c):
        state = low[c][...].reshape(hrows, blk)
        first = jnp.dot(hot_t[:, :hrows], state, preferred_element_type=F32)
        second = jnp.dot(hot_t[:, hrows:], state, preferred_element_type=F32)
        edge = first[:, :w] + second[:, w:]
        edges[s - 1][c][my_col] = jnp.concatenate([edge[:hb], edge[hb:]], axis=1).astype(BF16)
        for o in range(1, ncol):
            edge_copy(s, c, o).start()

    def interior_stage(s, c):
        for o in range(1, ncol):
            edge_copy(s, c, o).wait()
        parts = []
        for j in range(ncol):
            packed = edges[s - 1][c][j]
            parts += [packed[:, :w], packed[:, w:]]
        coupled = jnp.dot(cpl[...], jnp.concatenate(parts, axis=0), preferred_element_type=F32)
        both = jnp.concatenate(split_parts(coupled), axis=0)

        def load_rows(p, carry):
            for part in range(2):
                rows = pl.ds(pl.multiple_of(p * rows_each, rows_each), rows_each)
                full = pl.ds(pl.multiple_of(p * rows_each, rows_each) + part * hrows, rows_each)
                ones = hot[full, :]
                spread = jnp.dot(jnp.concatenate([ones, ones], axis=1), both, preferred_element_type=F32)
                pot = merged[c][rows, part * w:(part + 1) * w]
                given = src[full, c * w:(c + 1) * w].astype(F32)
                loaded[full, :] = (capb[full, :w] * pot + given + spread).astype(BF16)
            return carry

        lax.fori_loop(0, PIECES, load_rows, 0)

        def inner(p, carry):
            rows = pl.ds(pl.multiple_of(p * rows_each, rows_each), rows_each)
            under = pl.ds(pl.multiple_of(p * rows_each, rows_each) + hrows, rows_each)
            top = jnp.dot(inv[rows, :], loaded[...], preferred_element_type=F32)
            bottom = jnp.dot(inv[under, :], loaded[...], preferred_element_type=F32)
            value = jnp.concatenate([top, bottom], axis=1)
            merged[c][rows, :] = value
            low[c][pl.ds(p * per, per)] = value.astype(BF16).reshape(per, blk, blk)
            level_copy(s, 0, c, p).start()
            return carry

        lax.fori_loop(0, PIECES, inner, 0)

    def merge_stage(s, l, c):
        if s == 0 and c == 0:
            pan_loads[l].wait()
        for p in range(PIECES):
            level_copy(s, l, c, p).wait()
        final = s == STEPS - 1 and l == levels - 1
        for q in range(half):
            packed = got[s][l][c][q]
            tiles[q] = packed[:, :w]
            tiles[q + half] = packed[:, w:]

        def product(i):
            left = jnp.concatenate([pan[l, i, k] for k in range(kb)], axis=1)
            right = jnp.concatenate([tiles[pat_ref[0, 0, l, i, k]] for k in range(kb)], axis=0)
            return jnp.dot(left, right, preferred_element_type=F32)

        def piece(p, carry):
            for u in range(per):
                i = p * per + u
                rows = pl.ds(pl.multiple_of(i * blk, blk), blk)
                value = merged[c][rows, :] + jnp.concatenate([product(i), product(i + half)], axis=1)
                if final:
                    g, lane = c * w // blk, c * w % blk
                    under = pl.ds(pl.multiple_of(i * blk, blk) + hrows, blk)
                    outb[g, rows, lane:lane + w] = value[:, :w]
                    outb[g, under, lane:lane + w] = value[:, w:]
                else:
                    merged[c][rows, :] = value
                    low[c][i] = value.astype(BF16)
            if l < levels - 1:
                level_copy(s, l + 1, c, p).start()
            return carry

        lax.fori_loop(0, PIECES, piece, 0)

    done = set()
    first_step()
    for s, t, c in plan(levels, col_levels):
        if t == -2:
            gather_stage(s, c)
        elif t == -1:
            interior_stage(s, c)
        else:
            merge_stage(s, t, c)
        if s == STEPS - 1 and t == levels - 1:
            done.add(c)
            g = c * w // blk
            if all(k in done for k in range(CHUNKS) if k * w // blk == g):
                for p in range(PIECES):
                    out_copy(g, p).start()
    for g in range(rhs // blk):
        for p in range(PIECES):
            out_copy(g, p).wait()


def per_device(mesh, voltage, sources, capacity, inverse, couple, boundary, panels, pattern):
    ncol, nrow = mesh.shape["col"], mesh.shape["row"]
    _, _, levels, nb, kb, blk, _ = panels.shape
    ni, rhs = voltage.shape[2:]
    nbnd = boundary.shape[2]
    w = rhs // CHUNKS
    sems = pltpu.SemaphoreType.DMA
    scratch = [
        pltpu.VMEM((ni, ni), BF16),
        pltpu.VMEM((levels, nb, kb, blk, blk), BF16),
        pltpu.VMEM((nbnd, ncol * nbnd), BF16),
        pltpu.VMEM((ni, rhs), BF16),
        pltpu.VMEM((ni, rhs), BF16),
        pltpu.VMEM((ni, blk), F32),
        pltpu.VMEM((ni, nbnd), BF16),
        pltpu.VMEM((nbnd, ni), BF16),
        pltpu.VMEM((rhs // blk, ni, blk), F32),
        pltpu.VMEM((ni, rhs), BF16),
        pltpu.VMEM((ni, w), BF16),
        pltpu.VMEM((nb, blk, w), BF16),
        pltpu.VMEM((ncol, nbnd, rhs), BF16),
        sems((4 + levels,)),
        sems((rhs // blk, PIECES)),
        sems((STEPS, CHUNKS, ncol)),
        sems((STEPS, CHUNKS, ncol)),
        sems((STEPS, levels, CHUNKS, PIECES)),
        sems((STEPS, levels, CHUNKS, PIECES)),
    ]
    scratch += [pltpu.VMEM((ni // 2, blk), F32) for _ in range(CHUNKS)]
    scratch += [pltpu.VMEM((nb // 2, blk, blk), BF16) for _ in range(CHUNKS)]
    scratch += [pltpu.VMEM((ncol, nbnd // 2, 2 * w), BF16) for _ in range((STEPS - 1) * CHUNKS)]
    scratch += [pltpu.VMEM((nb // 2, blk, blk), BF16) for _ in range(STEPS * levels * CHUNKS)]
    vmem = pl.BlockSpec(memory_space=pltpu.VMEM)
    smem = pl.BlockSpec(memory_space=pltpu.SMEM)
    hbm = pl.BlockSpec(memory_space=pl.ANY)
    return pl.pallas_call(
        functools.partial(kernel, ncol, nrow, levels, nb, kb, blk, nbnd, rhs),
        out_shape=jax.ShapeDtypeStruct((1, 1, ni, rhs), F32),
        in_specs=[vmem, vmem, smem, hbm, hbm, hbm, hbm, hbm],
        out_specs=hbm,
        scratch_shapes=scratch,
        compiler_params=pltpu.CompilerParams(
            collective_id=0, has_side_effects=True, vmem_limit_bytes=67_043_328),
    )(capacity.reshape(1, ni), boundary.reshape(1, nbnd), pattern, voltage, sources, inverse, couple, panels)


def solution(mesh):
    return jax.shard_map(
        functools.partial(per_device, mesh),
        mesh=mesh,
        in_specs=(
            P("row", "col", None, None),
            P("row", "col", None, None),
            P("row", "col", None),
            P("row", "col", None, None),
            P("row", "col", None, None),
            P("row", "col", None),
            P("row", "col", None, None, None, None, None),
            P("row", "col", None, None, None),
        ),
        out_specs=P("row", "col", None, None),
        check_vma=False,
    )
```
